32 devices in a mesh: rep: 2 (over x), fsdp: 4 (over z), seq: 4 (over y, core).
Axes of the slice: x: 2, y: 2, z: 4, core: 2. Of those that a mesh axis runs over, the one named last changes fastest.
Arguments:
- images: bfloat16 [8, 512, 1024], P(('rep', 'fsdp'), 'seq'), may hold values from -6 to 6
- out_grad: bfloat16 [8, 512, 1024], P(('rep', 'fsdp'), 'seq'), may hold values from -6 to 6
- ln1_gain: bfloat16 [2, 1024], P(None, ('fsdp', 'seq')), may hold values from 0.5 to 1.5
- ln1_bias: bfloat16 [2, 1024], P(None, ('fsdp', 'seq')), may hold values from -4 to 4
- qkv_weight: bfloat16 [2, 1024, 3072], P(None, ('fsdp', 'seq')), may hold values from -0.25 to 0.25
- qv_bias: bfloat16 [2, 2, 1024], P(None, None, ('fsdp', 'seq')), may hold values from -4 to 4
- proj_weight: bfloat16 [2, 1024, 1024], P(None, ('fsdp', 'seq')), may hold values from -2 to 2
- proj_bias: bfloat16 [2, 1024], P(None, ('fsdp', 'seq')), may hold values from -4 to 4
- scale1: bfloat16 [2, 1024], P(None, ('fsdp', 'seq')), may hold values from 0.29882812 to 1.5
- ln2_gain: bfloat16 [2, 1024], P(None, ('fsdp', 'seq')), may hold values from 0.5 to 1.5
- ln2_bias: bfloat16 [2, 1024], P(None, ('fsdp', 'seq')), may hold values from -4 to 4
- fc1_weight: bfloat16 [2, 1024, 4096], P(None, ('fsdp', 'seq')), may hold values from -0.1875 to 0.1875
- fc1_bias: bfloat16 [2, 4096], P(None, ('fsdp', 'seq')), may hold values from -6 to 6
- fc2_weight: bfloat16 [2, 4096, 1024], P(None, ('fsdp', 'seq')), may hold values from -0.1875 to 0.1875
- fc2_bias: bfloat16 [2, 1024], P(None, ('fsdp', 'seq')), may hold values from -4 to 4
- scale2: bfloat16 [2, 1024], P(None, ('fsdp', 'seq')), may hold values from 0.29882812 to 1.5
Outputs:
- output: bfloat16 [8, 512, 1024], P(('rep', 'fsdp'), 'seq')
- input_grad: float32 [8, 512, 1024], P(('rep', 'fsdp'), 'seq')
- ln1_gain_grad: float32 [2, 1024], P(None, ('fsdp', 'seq'))
- ln1_bias_grad: float32 [2, 1024], P(None, ('fsdp', 'seq'))
- qkv_weight_grad: float32 [2, 1024, 3072], P(None, ('fsdp', 'seq'))
- qv_bias_grad: float32 [2, 2, 1024], P(None, None, ('fsdp', 'seq'))
- proj_weight_grad: float32 [2, 1024, 1024], P(None, ('fsdp', 'seq'))
- proj_bias_grad: float32 [2, 1024], P(None, ('fsdp', 'seq'))
- scale1_grad: float32 [2, 1024], P(None, ('fsdp', 'seq'))
- ln2_gain_grad: float32 [2, 1024], P(None, ('fsdp', 'seq'))
- ln2_bias_grad: float32 [2, 1024], P(None, ('fsdp', 'seq'))
- fc1_weight_grad: float32 [2, 1024, 4096], P(None, ('fsdp', 'seq'))
- fc1_bias_grad: float32 [2, 4096], P(None, ('fsdp', 'seq'))
- fc2_weight_grad: float32 [2, 4096, 1024], P(None, ('fsdp', 'seq'))
- fc2_bias_grad: float32 [2, 1024], P(None, ('fsdp', 'seq'))
- scale2_grad: float32 [2, 1024], P(None, ('fsdp', 'seq'))
The draws below stay inside these ranges and needn't reach their ends.
All inputs are finite; a program needn't handle non-finite values.
Results may differ from the reference program's by a relative error of at most 0.035.
Values may be sent and summed in bfloat16 or wider, within the bound.
No kernel may reach another device: no remote copies, remote signals or barrier semaphores. Data moves between devices by JAX's collectives and lax.ppermute only.
A program may use at most 256 MiB of HBM per device.

```python
import math
import jax
import jax.numpy as jnp
from jax import lax

D = 1024
HEADS = 16
HEAD_DIM = 64
FF = 4096
LAYERS = 2
SEQ = 512
IMAGES = 8


def block_scale(key, extent, cuts, least, high):
    def one(position, shards_of):
        draws = jax.random.uniform(jax.random.fold_in(jax.random.fold_in(key, 6), position), (shards_of,), jnp.float32, least / len(cuts), high / len(cuts))
        return jnp.repeat(jnp.exp(draws), extent[position] // shards_of).reshape((-1,) + (1,) * (len(extent) - position - 1))

    factor_of = one(*cuts[0])
    for cut in cuts[1:]:
        factor_of = factor_of * one(*cut)
    return factor_of


def scatter_about(rng, extent, scale, reach, split=(), held_as=jnp.bfloat16):
    drawn = jax.random.normal(rng, extent, jnp.float32) * scale
    if len(split) > 0:
        drawn = block_scale(rng, extent, split, -0.22, 0.18) * drawn
    return jnp.clip(drawn, min=-reach, max=reach).astype(held_as)


def setup_inputs(seed: int = 0) -> dict:
    arg_keys = jax.random.split(jax.random.key(seed), 17)
    return {
        "images": scatter_about(arg_keys[0], (IMAGES, SEQ, D), 1.0, 6.0, ((0, 8), (1, 4))),
        "out_grad": scatter_about(arg_keys[1], (IMAGES, SEQ, D), 1.0, 6.0, ((0, 8), (1, 4))),
        "ln1_gain": jnp.clip(1.0 + 0.1 * jax.random.normal(arg_keys[2], (LAYERS, D), jnp.float32), 0.5, 1.5).astype(jnp.bfloat16),
        "ln1_bias": scatter_about(arg_keys[3], (LAYERS, D), 0.3, 4.0, ((1, 16),)),
        "qkv_weight": scatter_about(arg_keys[4], (LAYERS, D, 3 * D), (D // 2) ** -0.5, 0.25, ((1, 16),)),
        "qv_bias": scatter_about(arg_keys[5], (LAYERS, 2, D), 0.3, 4.0, ((2, 16),)),
        "proj_weight": scatter_about(arg_keys[6], (LAYERS, D, D), (max(1, 4 * D // SEQ)) ** -0.5, 2.0, ((1, 16),)),
        "proj_bias": scatter_about(arg_keys[7], (LAYERS, D), 0.3, 4.0, ((1, 16),)),
        "scale1": jnp.clip(jnp.exp(math.log(1.5) - 1.6133518 * jax.random.uniform(arg_keys[8], (LAYERS, D), jnp.float32) ** block_scale(arg_keys[8], (LAYERS, D), ((1, 16),), -0.2, 0.2)), 0.29882812, 1.5).astype(jnp.bfloat16),
        "ln2_gain": jnp.clip(1.0 + 0.1 * jax.random.normal(arg_keys[9], (LAYERS, D), jnp.float32), 0.5, 1.5).astype(jnp.bfloat16),
        "ln2_bias": scatter_about(arg_keys[10], (LAYERS, D), 0.3, 4.0, ((1, 16),)),
        "fc1_weight": scatter_about(arg_keys[11], (LAYERS, D, FF), D ** -0.5, 0.1875, ((1, 16),)),
        "fc1_bias": scatter_about(arg_keys[12], (LAYERS, FF), 0.5, 6.0, ((1, 16),)),
        "fc2_weight": scatter_about(arg_keys[13], (LAYERS, FF, D), (FF // 4) ** -0.5, 0.1875, ((1, 16),)),
        "fc2_bias": scatter_about(arg_keys[14], (LAYERS, D), 0.3, 4.0, ((1, 16),)),
        "scale2": jnp.clip(jnp.exp(math.log(1.5) - 1.6133518 * jax.random.uniform(arg_keys[15], (LAYERS, D), jnp.float32) ** block_scale(arg_keys[15], (LAYERS, D), ((1, 16),), -0.2, 0.2)), 0.29882812, 1.5).astype(jnp.bfloat16),
    }


@jax.custom_vjp
def low(v):
    return lax.optimization_barrier(v.astype(jnp.bfloat16)).astype(jnp.float32)

@jax.custom_vjp
def low_back(v):
    return v

def low_keep(v):
    return (low(v), None)

def low_pass(kept, grad):
    return (grad,)

def back_keep(v):
    return (v, None)

def back_low(kept, grad):
    return (low(grad),)
low.defvjp(low_keep, low_pass)
low_back.defvjp(back_keep, back_low)
layer_eps = 1e-06

def norm_rows(values, gain_vec, shift_vec):
    center = values - lax.optimization_barrier(jnp.mean(values, axis=-1, keepdims=True))
    spread = lax.optimization_barrier(jnp.mean(center * center, axis=-1, keepdims=True))
    return center * lax.rsqrt(spread + layer_eps) * gain_vec + shift_vec

def product(left, right):
    return jnp.dot(left, right, precision=lax.Precision.HIGHEST)

def attend_block(query_block, keys_img, values_img):
    score_scale = 1.0 / math.sqrt(HEAD_DIM)
    scores = jnp.einsum('qhd,khd->hqk', query_block, keys_img, precision=lax.Precision.HIGHEST) * score_scale
    scores = low_back(scores)
    weights = jax.nn.softmax(scores, axis=-1)
    return jnp.einsum('hqk,khd->qhd', low(weights), values_img, precision=lax.Precision.HIGHEST)

def attend_image(queries, keys_img, values_img):
    block_rows = math.gcd(SEQ, 512)
    blocks = queries.reshape(SEQ // block_rows, block_rows, HEADS, HEAD_DIM)

    def one_block(query_block):
        return attend_block(query_block, keys_img, values_img)
    return lax.map(jax.checkpoint(one_block), blocks).reshape(SEQ, HEADS, HEAD_DIM)

def block_layer(stream, params):
    gain_one, shift_one, qkv_w, qv_b, proj_w, proj_b, scale_one, gain_two, shift_two, fc1_w, fc1_b, fc2_w, fc2_b, scale_two = params
    image_count = stream.shape[0]
    normed = low(norm_rows(stream, gain_one, shift_one))
    mixed = product(normed, qkv_w)
    queries = low(low_back(mixed[..., :D] + qv_b[0]))
    keys_all = low(low_back(mixed[..., D:2 * D]))
    values_all = low(low_back(mixed[..., 2 * D:] + qv_b[1]))
    head_shape = (image_count, SEQ, HEADS, HEAD_DIM)
    attended = jax.vmap(attend_image)(queries.reshape(head_shape), keys_all.reshape(head_shape), values_all.reshape(head_shape))
    attended = low(low_back(attended.reshape(image_count, SEQ, D)))
    branch_one = low_back(product(attended, proj_w) + proj_b)
    middle = stream + scale_one * branch_one
    normed_two = low(norm_rows(middle, gain_two, shift_two))
    hidden_pre = low_back(product(normed_two, fc1_w) + fc1_b)
    hidden_act = low(jax.nn.gelu(hidden_pre, approximate=False))
    branch_two = low_back(product(hidden_act, fc2_w) + fc2_b)
    return middle + scale_two * branch_two

def reference(images, out_grad, ln1_gain, ln1_bias, qkv_weight, qv_bias, proj_weight, proj_bias, scale1, ln2_gain, ln2_bias, fc1_weight, fc1_bias, fc2_weight, fc2_bias, scale2):
    params = tuple((param_arr.astype(jnp.float32) for param_arr in (ln1_gain, ln1_bias, qkv_weight, qv_bias, proj_weight, proj_bias, scale1, ln2_gain, ln2_bias, fc1_weight, fc1_bias, fc2_weight, fc2_bias, scale2)))
    group_size = math.gcd(IMAGES, max(1, 4096 // SEQ))
    inputs = images.reshape(IMAGES // group_size, group_size, SEQ, D)
    cotangents = out_grad.reshape(IMAGES // group_size, group_size, SEQ, D)

    def forward(stream, weights):
        for layer_index in range(LAYERS):
            stream = block_layer(stream, tuple((item[layer_index] for item in weights)))
        return stream

    def step(totals, pair):
        batch_in, batch_cot = pair
        result, pull = jax.vjp(forward, batch_in.astype(jnp.float32), params)
        stream_grad, param_grads = pull(batch_cot.astype(jnp.float32))
        totals = tuple((total_arr + grad_arr for total_arr, grad_arr in zip(totals, param_grads)))
        return (totals, (result.astype(jnp.bfloat16), stream_grad))
    start = tuple((jnp.zeros_like(item) for item in params))
    totals, (outputs, input_grads) = lax.scan(step, start, (inputs, cotangents))
    return (outputs.reshape(IMAGES, SEQ, D), input_grads.reshape(IMAGES, SEQ, D), totals[0], totals[1], totals[2], totals[3], totals[4], totals[5], totals[6], totals[7], totals[8], totals[9], totals[10], totals[11], totals[12], totals[13])
```

```python
from functools import partial
import math

import jax
import jax.numpy as jnp
from jax import lax
from jax.experimental import pallas as pl
from jax.experimental.pallas import tpu as pltpu
from jax.sharding import PartitionSpec as P

HEADS = 16
HEAD_DIM = 64
LAYERS = 2
EPS = 1e-06
F32 = jnp.float32
BF16 = jnp.bfloat16
VECTORS = 8


class Plan:
    def __init__(self, mesh):
        self.rep = mesh.shape["rep"]
        self.fsdp = mesh.shape["fsdp"]
        self.seq = mesh.shape["seq"]
        self.pairs = self.seq == 4
        self.fast = self.rep == 2 and self.fsdp == 4 and self.seq == 4

    def swap(self, value, axis, bits):
        size = getattr(self, axis)
        return lax.ppermute(value, axis, [(i, i ^ bits) for i in range(size)])

    def seq_gather(self, block):
        if not self.pairs:
            parts = lax.all_gather(block, "seq", axis=0)
            return [parts[i] for i in range(self.seq)]
        far = self.swap(block, "seq", 2)
        near = self.swap(block, "seq", 1)
        last = self.swap(far, "seq", 1)
        return [block, near, far, last]

    def seq_scatter(self, parts):
        if not self.pairs:
            stacked = jnp.stack([p.astype(BF16) for p in parts])
            return lax.psum_scatter(stacked, "seq", scatter_dimension=0, tiled=False).astype(F32)
        far_own, far_near = parts[2], parts[3]
        got_far = self.swap(far_near.astype(BF16), "seq", 1)
        got_own = self.swap(parts[1].astype(BF16), "seq", 1)
        send = (far_own.astype(F32) + got_far.astype(F32)).astype(BF16)
        got = self.swap(send, "seq", 2)
        return parts[0].astype(F32) + got_own.astype(F32) + got.astype(F32)


def after(value, *others):
    return lax.optimization_barrier((value,) + others)[0]


def fetch_columns(local, groups, plan):
    full = lax.all_gather(local, ("fsdp", "seq"), axis=0, tiled=True)
    total = full.shape[0]
    view = full.reshape(total, groups, plan.seq, -1)
    mine = lax.dynamic_index_in_dim(view, lax.axis_index("seq"), 2, keepdims=False)
    return mine.reshape(total, -1)


def fetch_rows(local, plan):
    rows, cols = local.shape
    full = lax.all_gather(local, ("fsdp", "seq"), axis=0, tiled=True)
    return lax.dynamic_slice_in_dim(
        full, lax.axis_index("seq") * (rows * plan.fsdp), rows * plan.fsdp, 0
    )


def give_columns(grad, groups, plan):
    total, cols = grad.shape
    view = grad.astype(BF16).reshape(total, groups, 1, cols // groups)
    wide = jnp.zeros((total, groups, plan.seq, cols // groups), BF16)
    wide = lax.dynamic_update_slice(wide, view, (0, 0, lax.axis_index("seq"), 0))
    part = lax.psum_scatter(
        wide.reshape(total, -1), ("fsdp", "seq"), scatter_dimension=0, tiled=True
    )
    return lax.psum(part, "rep").astype(F32)


def give_rows(grad, plan):
    total, cols = grad.shape
    wide = jnp.zeros((plan.seq * total, cols), BF16)
    wide = lax.dynamic_update_slice(wide, grad.astype(BF16), (lax.axis_index("seq") * total, 0))
    part = lax.psum_scatter(wide, ("fsdp", "seq"), scatter_dimension=0, tiled=True)
    return lax.psum(part, "rep").astype(F32)


def across(value, axis):
    return lax.all_to_all(value, axis, split_axis=0, concat_axis=0, tiled=True)


def to_all(block, plan):
    return lax.all_gather(block, "fsdp", axis=0)


def twin_swap(value):
    return lax.ppermute(value, "rep", [(0, 1), (1, 0)])


def pick(value, axis, index):
    return lax.dynamic_index_in_dim(value, index, axis, keepdims=False)


def fetch_fast(params, plan):
    twin = lax.axis_index("rep")
    qkv, proj, fc1, fc2 = params
    rows, wide = qkv.shape[1], proj.shape[2]
    seq, fsdp = plan.seq, plan.fsdp

    def qkv_piece(local):
        view = local.reshape(rows, 3, 2, fsdp // 2, seq, -1)
        return pick(view, 2, twin).transpose(3, 0, 1, 2, 4).reshape(seq, rows, -1)

    def fc1_piece(local):
        view = local.reshape(rows, fsdp, seq, 2, -1)
        return pick(view, 3, twin).transpose(2, 0, 1, 3).reshape(seq, rows, -1)

    first = across(qkv_piece(qkv[0]), "seq")
    rest = [fc1_piece(fc1[0]), qkv_piece(qkv[1]), fc1_piece(fc1[1])]
    cut = [rest[0].shape[2], rest[0].shape[2] + rest[1].shape[2]]
    rest = across(after(jnp.concatenate(rest, axis=2), first), "seq")
    qkv_own = [first, rest[:, :, cut[0] : cut[1]]]
    fc1_own = [rest[:, :, : cut[0]], rest[:, :, cut[1] :]]

    out = []
    done = None
    for layer in range(LAYERS):
        half = pick(fc2[layer].reshape(2, -1, wide), 0, twin)
        got = []
        for block in (qkv_own[layer], proj[layer], fc1_own[layer], half):
            done = to_all(block, plan)
            got.append(done)
        proj_w = got[1]
        proj_w = jnp.where(twin == 0, proj_w, jnp.roll(proj_w, fsdp // 2, axis=0)).reshape(-1, wide)
        mine = [
            got[0].reshape(fsdp * seq * rows, -1),
            got[2].reshape(fsdp * seq * rows, -1),
            got[3].reshape(-1, wide),
        ]
        theirs = [twin_swap(m) for m in mine]
        out.append((mine[0], theirs[0], proj_w, mine[1], theirs[1], mine[2], theirs[2]))
    return out


def give_half(mine, theirs):
    got = twin_swap(theirs)
    both = (mine.astype(F32) + got.astype(F32)).astype(BF16)
    both = both.reshape((4, -1) + both.shape[1:])
    return lax.psum_scatter(both, "fsdp", scatter_dimension=0, tiled=False)


def give_fast(grads, plan):
    qkv_m, qkv_t, proj_g, fc1_m, fc1_t, fc2_m, fc2_t = grads
    twin = lax.axis_index("rep")
    seq = plan.seq
    fc2_h = give_half(fc2_m, fc2_t)
    fc1_h = give_half(fc1_m, fc1_t)
    fc1_h = across(fc1_h.reshape((seq, -1) + fc1_h.shape[1:]), "seq")
    proj_g = proj_g.reshape((plan.fsdp, -1) + proj_g.shape[1:])
    proj_g = jnp.where(twin == 0, proj_g, jnp.roll(proj_g, plan.fsdp // 2, axis=0))
    proj_h = jnp.sum(across(proj_g, "fsdp").astype(F32), axis=0).astype(BF16)
    qkv_h = give_half(qkv_m, qkv_t)
    qkv_h = across(qkv_h.reshape((seq, -1) + qkv_h.shape[1:]), "seq")
    return [(h, twin_swap(h)) for h in (qkv_h, proj_h, fc1_h, fc2_h)]


def finish(kind, shape, parts):
    twin = lax.axis_index("rep").astype(jnp.int32).reshape(1)

    def kernel(where, *refs):
        out = refs[-1]
        for layer in range(LAYERS):
            mine, theirs = refs[2 * layer], refs[2 * layer + 1]
            if kind == "sum":
                out[layer] = mine[...].astype(F32) + theirs[...].astype(F32)
                continue
            first = where[0] == 0
            for h in (0, 1):
                keep = first if h == 0 else jnp.logical_not(first)
                if kind == "rows":
                    rows = mine.shape[0]
                    got = jnp.where(keep, mine[...].astype(F32), theirs[...].astype(F32))
                    out[layer, h * rows : (h + 1) * rows, :] = got
                elif kind == "fc1":
                    for z in range(4):
                        for s in range(4):
                            lanes = slice(z * 128, (z + 1) * 128)
                            got = jnp.where(
                                keep, mine[s, :, lanes].astype(F32), theirs[s, :, lanes].astype(F32)
                            )
                            at = ((z * 4 + s) * 2 + h) * 128
                            out[layer, :, at : at + 128] = got
                else:
                    for j in range(3):
                        wide = [
                            jnp.where(
                                keep,
                                mine[s, :, j * 128 : j * 128 + 128].astype(F32),
                                theirs[s, :, j * 128 : j * 128 + 128].astype(F32),
                            )
                            for s in range(4)
                        ]
                        for i in (0, 1):
                            piece = [w[:, i * 64 : i * 64 + 64] for w in wide]
                            at = (j * 4 + 2 * h + i) * 256
                            out[layer, :, at : at + 256] = jnp.concatenate(piece, axis=1)

    flat = [x for pair in parts for x in pair]
    return pl.pallas_call(
        kernel,
        grid_spec=pltpu.PrefetchScalarGridSpec(
            num_scalar_prefetch=1,
            grid=(),
            in_specs=[pl.BlockSpec(memory_space=pltpu.VMEM)] * len(flat),
            out_specs=pl.BlockSpec(memory_space=pltpu.VMEM),
        ),
        out_shape=jax.ShapeDtypeStruct(shape, F32),
        name="finish_" + kind,
    )(twin, *flat)


def owned(full, groups, plan):
    if plan.fast:
        view = full.reshape(groups, plan.fsdp, plan.seq, -1)
        mine = lax.dynamic_index_in_dim(view, lax.axis_index("seq"), 2, keepdims=False)
    else:
        view = full.reshape(groups, plan.seq, -1)
        mine = lax.dynamic_index_in_dim(view, lax.axis_index("seq"), 1, keepdims=False)
    return mine.reshape(groups, -1)


def spread(mine, groups, plan):
    if plan.fast:
        view = mine.reshape(groups, plan.fsdp, 1, -1)
        full = jnp.zeros((groups, plan.fsdp, plan.seq, view.shape[-1]), F32)
        full = lax.dynamic_update_slice(full, view, (0, 0, lax.axis_index("seq"), 0))
    else:
        view = mine.reshape(groups, 1, -1)
        full = jnp.zeros((groups, plan.seq, view.shape[-1]), F32)
        full = lax.dynamic_update_slice(full, view, (0, lax.axis_index("seq"), 0))
    return full.reshape(groups, -1)


def norm_stats(values):
    center = values - jnp.mean(values, axis=-1, keepdims=True)
    scale = lax.rsqrt(jnp.mean(center * center, axis=-1, keepdims=True) + EPS)
    return center * scale, scale


def norm_back(xhat, scale, grad, gain):
    e = grad * gain
    return scale * (
        e - jnp.mean(e, axis=-1, keepdims=True) - xhat * jnp.mean(e * xhat, axis=-1, keepdims=True)
    )


ROWS = 128
ROOT = 1.0 / math.sqrt(HEAD_DIM)


def run(kernel, name, outs, args, flops, scratch=()):
    spec = pl.BlockSpec(memory_space=pltpu.VMEM)
    moved = sum(x.size * x.dtype.itemsize for x in args) + sum(
        math.prod(o.shape) * o.dtype.itemsize for o in outs
    )
    return pl.pallas_call(
        kernel,
        in_specs=[spec] * len(args),
        out_specs=[spec] * len(outs),
        out_shape=outs,
        scratch_shapes=list(scratch),
        compiler_params=pltpu.CompilerParams(vmem_limit_bytes=48 * 1024 * 1024),
        cost_estimate=pl.CostEstimate(flops=flops, bytes_accessed=moved, transcendentals=0),
        name=name,
    )(*args)


def shape_of(dims, dtype=BF16):
    return jax.ShapeDtypeStruct(dims, dtype)


def nn(a, b):
    return jnp.dot(a, b, preferred_element_type=F32)


def nt(a, b):
    return lax.dot_general(a, b, (((1,), (1,)), ((), ())), preferred_element_type=F32)


def tn(a, b):
    return nn(a.T, b)


def attend(blocks, qkv_w, qv_b, proj_w):
    count = len(blocks)
    wide = proj_w.shape[1]
    third = qkv_w[0].shape[1] // 3
    own = 2 * third
    total = count * ROWS

    def kernel(*refs):
        n = refs[:count]
        wm, wt, bias, proj = refs[count : count + 4]
        outs = refs[count + 4 :]
        p, (q, k, v, att) = outs[:count], outs[count:]
        for b in range(count):
            rows = slice(b * ROWS, (b + 1) * ROWS)
            x = n[b][...]
            for i, w in enumerate((wm, wt)):
                mixed = nn(x, w[...])
                cols = slice(i * third, (i + 1) * third)
                q[rows, cols] = (mixed[:, :third] + bias[0:1, cols]).astype(BF16)
                k[rows, cols] = mixed[:, third : 2 * third].astype(BF16)
                v[rows, cols] = (mixed[:, 2 * third :] + bias[1:2, cols]).astype(BF16)
        for pair in range(own // 128):
            lanes = slice(pair * 128, (pair + 1) * 128)
            k2, v2 = k[:, lanes], v[:, lanes]

            def block(b, _):
                rows = pl.ds(pl.multiple_of(b * ROWS, ROWS), ROWS)
                q2 = q[rows, lanes]
                got = []
                for h in range(2):
                    part = slice(h * HEAD_DIM, (h + 1) * HEAD_DIM)
                    scores = nt(q2[:, part], k2[:, part]) * ROOT
                    high = jnp.max(scores, axis=1, keepdims=True)
                    exped = jnp.exp(scores - high)
                    inv = 1.0 / jnp.sum(exped, axis=1, keepdims=True)
                    got.append(nn((exped * inv).astype(BF16), v2[:, part]))
                att[rows, lanes] = jnp.concatenate(got, axis=1).astype(BF16)
                return 0

            lax.fori_loop(0, count, block, 0)
        for b in range(count):
            rows = slice(b * ROWS, (b + 1) * ROWS)
            p[b][...] = nn(att[rows, :], proj[...]).astype(BF16)

    outs = [shape_of((ROWS, wide))] * count + [shape_of((total, own))] * 4
    flops = 2 * total * wide * own * 4 + 4 * total * total * own
    got = run(kernel, "attend", outs, (*blocks, *qkv_w, qv_b, proj_w), flops)
    return got[:count], got[count:]


def attend_back(grads, qkv_w, proj_w, saved):
    query, key, value = saved
    count = len(grads)
    wide = proj_w.shape[1]
    third = qkv_w[0].shape[1] // 3
    own = 2 * third
    total = count * ROWS

    def kernel(*refs):
        g = refs[:count]
        wm, wt, proj, q, k, v = refs[count : count + 6]
        outs = refs[count + 6 :]
        p, (mm, mt, sums, ag, dk, dv) = outs[:count], outs[count:]
        for b in range(count):
            ag[b * ROWS : (b + 1) * ROWS, :] = nt(g[b][...], proj[...]).astype(BF16)
        for pair in range(own // 128):
            lanes = slice(pair * 128, (pair + 1) * 128)
            out = (mm, mt)[pair * 128 // third]
            base = pair * 128 % third
            k2, v2 = k[:, lanes], v[:, lanes]
            dk[...] = jnp.zeros_like(dk)
            dv[...] = jnp.zeros_like(dv)

            def block(b, _):
                rows = pl.ds(pl.multiple_of(b * ROWS, ROWS), ROWS)
                q2, a2 = q[rows, lanes], ag[rows, lanes]
                dq2, dk2, dv2 = [], [], []
                for h in range(2):
                    part = slice(h * HEAD_DIM, (h + 1) * HEAD_DIM)
                    qh, ah, kh, vh = q2[:, part], a2[:, part], k2[:, part], v2[:, part]
                    scores = nt(kh, qh) * ROOT
                    high = jnp.max(scores, axis=0, keepdims=True)
                    exped = jnp.exp(scores - high)
                    probs = exped * (1.0 / jnp.sum(exped, axis=0, keepdims=True))
                    pg = nt(vh, ah)
                    center = jnp.sum(probs * pg, axis=0, keepdims=True)
                    sg = (probs * (pg - center)).astype(BF16)
                    dk2.append(nn(sg, qh))
                    dv2.append(nn(probs.astype(BF16), ah))
                    dq2.append(tn(sg, kh))
                dk[...] += jnp.concatenate(dk2, axis=1)
                dv[...] += jnp.concatenate(dv2, axis=1)
                dq = (jnp.concatenate(dq2, axis=1) * ROOT).astype(BF16)
                out[rows, base : base + 128] = dq
                return 0

            lax.fori_loop(0, count, block, 0)
            out[:, third + base : third + base + 128] = (dk[...] * ROOT).astype(BF16)
            out[:, 2 * third + base : 2 * third + base + 128] = dv[...].astype(BF16)
        for i, m in enumerate((mm, mt)):
            cols = slice(i * third, (i + 1) * third)
            for j, at in enumerate((0, 2 * third)):
                part = m[:, at : at + third].astype(F32)
                sums[j : j + 1, cols] = jnp.sum(part, axis=0, keepdims=True)
        for b in range(count):
            rows = slice(b * ROWS, (b + 1) * ROWS)
            p[b][...] = (nt(mm[rows, :], wm[...]) + nt(mt[rows, :], wt[...])).astype(BF16)

    outs = [shape_of((ROWS, wide))] * count + [shape_of((total, 3 * third))] * 2
    outs.append(shape_of((2, own), F32))
    flops = 2 * total * wide * own * 4 + 10 * total * total * own
    args = (*grads, *qkv_w, proj_w, query, key, value)
    scratch = [pltpu.VMEM((total, own), BF16)] + [pltpu.VMEM((total, 128), F32)] * 2
    got = run(kernel, "attend_back", outs, args, flops, scratch)
    return got[:count], got[count : count + 2], got[count + 2]


def mlp(blocks, fc1_w, fc1_b, fc2_w):
    count = len(blocks)
    wide, width = fc1_w[0].shape
    total = count * ROWS

    def kernel(*refs):
        n = refs[:count]
        wins, bias, wouts = refs[count : count + 2], refs[count + 2], refs[count + 3 : count + 5]
        outs = refs[count + 5 :]
        p, hidden, slope = outs[:count], outs[count : count + 2], outs[count + 2 :]
        for b in range(count):
            rows = slice(b * ROWS, (b + 1) * ROWS)
            x = n[b][...]
            acc = None
            for i in range(2):
                u = nn(x, wins[i][...]) + bias[i : i + 1, :]
                phi = 0.5 + 0.5 * lax.erf(u * math.sqrt(0.5))
                h = (u * phi).astype(BF16)
                bell = jnp.exp(u * u * -0.5) * (1.0 / math.sqrt(2.0 * math.pi))
                hidden[i][rows, :] = h
                slope[i][rows, :] = (phi + u * bell).astype(BF16)
                part = nn(h, wouts[i][...])
                acc = part if acc is None else acc + part
            p[b][...] = acc.astype(BF16)

    outs = [shape_of((ROWS, wide))] * count + [shape_of((total, width))] * 4
    args = (*blocks, *fc1_w, jnp.stack(fc1_b), *fc2_w)
    got = run(kernel, "mlp", outs, args, 8 * total * wide * width)
    return got[:count], got[count : count + 2], got[count + 2 :]


def mlp_back(grads, slope, fc1_w, fc2_w):
    count = len(grads)
    wide, width = fc1_w[0].shape
    total = count * ROWS

    def kernel(*refs):
        g = refs[:count]
        slopes, wins, wouts = [refs[count + 2 * i : count + 2 * i + 2] for i in range(3)]
        outs = refs[count + 6 :]
        p, pre, sums = outs[:count], outs[count : count + 2], outs[count + 2]
        for b in range(count):
            rows = slice(b * ROWS, (b + 1) * ROWS)
            x = g[b][...]
            acc = None
            for i in range(2):
                low = (nt(x, wouts[i][...]) * slopes[i][rows, :].astype(F32)).astype(BF16)
                pre[i][rows, :] = low
                part_sum = jnp.sum(low.astype(F32), axis=0, keepdims=True)
                if b == 0:
                    sums[i : i + 1, :] = part_sum
                else:
                    sums[i : i + 1, :] += part_sum
                part = nt(low, wins[i][...])
                acc = part if acc is None else acc + part
            p[b][...] = acc.astype(BF16)

    outs = [shape_of((ROWS, wide))] * count + [shape_of((total, width))] * 2
    outs.append(shape_of((2, width), F32))
    args = (*grads, *slope, *fc1_w, *fc2_w)
    got = run(kernel, "mlp_back", outs, args, 8 * total * wide * width)
    return got[:count], got[count : count + 2], got[count + 2]


def outer(lefts, blocks, name):
    count = len(blocks)
    wide = blocks[0].shape[1]
    total = count * ROWS

    def kernel(*refs):
        left, right = refs[: len(lefts)], refs[len(lefts) : len(lefts) + count]
        outs, whole = refs[len(lefts) + count : -1], refs[-1]
        for b in range(count):
            whole[b * ROWS : (b + 1) * ROWS, :] = right[b][...]
        for ref, out in zip(left, outs):
            for at in range(0, ref.shape[1], 128):
                out[at : at + 128, :] = tn(ref[:, at : at + 128], whole[...]).astype(BF16)

    outs = [shape_of((x.shape[1], wide)) for x in lefts]
    flops = 2 * total * wide * sum(x.shape[1] for x in lefts)
    scratch = [pltpu.VMEM((total, wide), BF16)]
    return run(kernel, name, outs, (*lefts, *blocks), flops, scratch)


def outer_rows(blocks, rights, name):
    count = len(blocks)
    wide = blocks[0].shape[1]
    total = count * ROWS

    def kernel(*refs):
        left, right = refs[:count], refs[count : count + len(rights)]
        outs, whole = refs[count + len(rights) : -1], refs[-1]
        for b in range(count):
            whole[b * ROWS : (b + 1) * ROWS, :] = left[b][...]
        for at in range(0, wide, 128):
            turned = whole[:, at : at + 128].T
            for ref, out in zip(right, outs):
                out[at : at + 128, :] = nn(turned, ref[...]).astype(BF16)

    outs = [shape_of((wide, x.shape[1])) for x in rights]
    flops = 2 * total * wide * sum(x.shape[1] for x in rights)
    scratch = [pltpu.VMEM((total, wide), BF16)]
    return run(kernel, name, outs, (*blocks, *rights), flops, scratch)


def layer_forward(stream, weights, vecs, qv_b, fc1_b, plan):
    qkv_w, proj_w, fc1_w, fc2_w = weights
    gain_one, shift_one, proj_b, scale_one, gain_two, shift_two, fc2_b, scale_two = vecs
    xhat, _ = norm_stats(stream)
    normed = plan.seq_gather((xhat * gain_one + shift_one).astype(BF16))
    parts, heads = attend(normed, qkv_w, qv_b, proj_w)
    branch_one = plan.seq_scatter(parts) + proj_b
    middle = stream + scale_one * branch_one
    xhat_two, _ = norm_stats(middle)
    normed_two = plan.seq_gather((xhat_two * gain_two + shift_two).astype(BF16))
    parts, hidden, slope = mlp(normed_two, fc1_w, fc1_b, fc2_w)
    branch_two = plan.seq_scatter(parts) + fc2_b
    result = middle + scale_two * branch_two
    saved = (
        stream, normed, heads, branch_one, middle, normed_two, hidden, slope, branch_two,
    )
    return result, saved


def layer_backward(grad, saved, weights, vecs, plan):
    stream, normed, heads, branch_one, middle, normed_two, hidden, slope, branch_two = saved
    qkv_w, proj_w, fc1_w, fc2_w = weights
    gain_one, shift_one, proj_b, scale_one, gain_two, shift_two, fc2_b, scale_two = vecs
    grad_two = (scale_two * grad).astype(BF16)
    scale_two_grad = jnp.sum(grad * branch_two, axis=0)
    fc2_b_grad = jnp.sum(grad_two.astype(F32), axis=0)
    grad_two_all = plan.seq_gather(grad_two)
    parts, pre_grad, fc1_b_grad = mlp_back(grad_two_all, slope, fc1_w, fc2_w)
    normed_two_grad = plan.seq_scatter(parts)
    fc2_w_grad = outer(hidden, grad_two_all, "fc2_grad")
    fc1_w_grad = outer_rows(normed_two, pre_grad, "fc1_grad")
    xhat_two, s_two = norm_stats(middle)
    gain_two_grad = jnp.sum(normed_two_grad * xhat_two, axis=0)
    shift_two_grad = jnp.sum(normed_two_grad, axis=0)
    middle_grad = grad + norm_back(xhat_two, s_two, normed_two_grad, gain_two)
    scale_one_grad = jnp.sum(middle_grad * branch_one, axis=0)
    grad_one = (scale_one * middle_grad).astype(BF16)
    proj_b_grad = jnp.sum(grad_one.astype(F32), axis=0)
    grad_one_all = plan.seq_gather(grad_one)
    parts, mixed_grad, qv_b_grad = attend_back(grad_one_all, qkv_w, proj_w, heads[:3])
    normed_grad = plan.seq_scatter(parts)
    (proj_w_grad,) = outer(heads[3:], grad_one_all, "proj_grad")
    qkv_w_grad = outer_rows(normed, mixed_grad, "qkv_grad")
    xhat, s_one = norm_stats(stream)
    gain_one_grad = jnp.sum(normed_grad * xhat, axis=0)
    shift_one_grad = jnp.sum(normed_grad, axis=0)
    stream_grad = middle_grad + norm_back(xhat, s_one, normed_grad, gain_one)
    vec_grads = jnp.stack(
        [
            gain_one_grad, shift_one_grad, proj_b_grad, scale_one_grad,
            gain_two_grad, shift_two_grad, fc2_b_grad, scale_two_grad,
        ]
    )
    if plan.fast:
        weight_grads = give_fast((*qkv_w_grad, proj_w_grad, *fc1_w_grad, *fc2_w_grad), plan)
    else:
        weight_grads = (
            give_columns(join_columns(qkv_w_grad, 3), 3, plan),
            give_rows(proj_w_grad, plan),
            give_columns(join_columns(fc1_w_grad, 1), 1, plan),
            give_rows(jnp.concatenate(fc2_w_grad, axis=0), plan),
        )
    return stream_grad, weight_grads, (vec_grads, qv_b_grad, fc1_b_grad)


def split_columns(value, groups):
    view = value.reshape(value.shape[0], groups, 2, -1)
    return [view[:, :, i].reshape(value.shape[0], -1) for i in (0, 1)]


def join_columns(halves, groups):
    rows = halves[0].shape[0]
    views = [h.reshape(rows, groups, 1, -1) for h in halves]
    return jnp.concatenate(views, axis=2).reshape(rows, -1)


def by_twin(value, plan):
    twin = lax.axis_index("rep")
    return jnp.where(twin == 0, value, jnp.roll(value, value.shape[-1] // 2, axis=-1))


def halves_of(value, plan):
    twin = lax.axis_index("rep")
    lead = value.shape[:-3]
    return [pick(value, value.ndim - 2, i).reshape(lead + (-1,)) for i in (twin, 1 - twin)]


def shards(
    plan, images, out_grad, ln1_gain, ln1_bias, qkv_weight, qv_bias, proj_weight, proj_bias,
    scale1, ln2_gain, ln2_bias, fc1_weight, fc1_bias, fc2_weight, fc2_bias, scale2,
):
    parts = plan.fsdp * plan.seq
    vectors = jnp.stack(
        [ln1_gain, ln1_bias, proj_bias, scale1, ln2_gain, ln2_bias, fc2_bias, scale2], axis=1
    )
    small = vectors.shape[2]
    packed = jnp.concatenate(
        [vectors.reshape(LAYERS, -1), qv_bias.reshape(LAYERS, -1), fc1_bias], axis=1
    )
    both = ("fsdp", "seq")
    if plan.fast:
        spread_out = jnp.broadcast_to(packed.reshape(1, -1, 128), (parts, packed.size // 128, 128))
        gathered = lax.all_to_all(spread_out, both, split_axis=0, concat_axis=0, tiled=True)
        gathered = gathered.reshape(parts, LAYERS, -1).astype(F32)
    else:
        gathered = lax.all_gather(packed, both, axis=0).astype(F32)
    gathered = gathered.transpose(1, 0, 2)
    cut_one = VECTORS * small
    cut_two = cut_one + 2 * small
    vecs, qv_bs, fc1_bs = [], [], []
    for layer in range(LAYERS):
        g = gathered[layer]
        vec = g[:, :cut_one].reshape(parts, VECTORS, small).transpose(1, 0, 2)
        vecs.append(list(vec.reshape(VECTORS, -1)))
        qv = g[:, cut_one:cut_two].reshape(parts, 2, small).transpose(1, 0, 2).reshape(2, -1)
        qv = owned(qv.reshape(-1), 2, plan)
        fc1_own = owned(g[:, cut_two:].reshape(-1), 1, plan)[0]
        if plan.fast:
            qv = by_twin(qv, plan)
            fc1_bs.append(halves_of(fc1_own.reshape(plan.fsdp, 2, -1), plan))
        else:
            fc1_bs.append(list(fc1_own.reshape(2, -1)))
        qv_bs.append(qv)

    if plan.fast:
        fetched = fetch_fast((qkv_weight, proj_weight, fc1_weight, fc2_weight), plan)
        weights = [(w[0:2], w[2], w[3:5], w[5:7]) for w in fetched]
    else:
        weights = [
            (
                split_columns(fetch_columns(qkv_weight[layer], 3, plan), 3),
                fetch_rows(proj_weight[layer], plan),
                split_columns(fetch_columns(fc1_weight[layer], 1, plan), 1),
                jnp.split(fetch_rows(fc2_weight[layer], plan), 2),
            )
            for layer in range(LAYERS)
        ]
    stream = images[0].astype(F32)
    saved = []
    for layer in range(LAYERS):
        stream, keep = layer_forward(
            stream, weights[layer], vecs[layer], qv_bs[layer], fc1_bs[layer], plan
        )
        saved.append(keep)
    output = stream.astype(BF16)[None]
    grad = out_grad[0].astype(F32)
    weight_grads = [None] * LAYERS
    small_grads = [None] * LAYERS
    for layer in reversed(range(LAYERS)):
        grad, weight_grads[layer], smalls = layer_backward(
            grad, saved[layer], weights[layer], vecs[layer], plan
        )
        vec_grads, qv_b_grad, fc1_b_grad = smalls
        if plan.fast:
            twin = lax.axis_index("rep")
            qv_b_grad = by_twin(qv_b_grad, plan)
            mine, theirs = [t.reshape(plan.fsdp, 1, -1) for t in fc1_b_grad]
            first = jnp.where(twin == 0, mine, theirs)
            second = jnp.where(twin == 0, theirs, mine)
            fc1_b_grad = jnp.concatenate([first, second], axis=1).reshape(-1)
        else:
            fc1_b_grad = fc1_b_grad.reshape(-1)
        qv_full = spread(qv_b_grad, 2, plan).reshape(2, parts, small).transpose(1, 0, 2)
        fc1_full = spread(fc1_b_grad[None], 1, plan).reshape(parts, -1)
        vec_full = vec_grads.reshape(VECTORS, parts, small).transpose(1, 0, 2)
        whole = jnp.concatenate(
            [vec_full.reshape(parts, -1), qv_full.reshape(parts, -1), fc1_full], axis=1
        )
        if plan.fast:
            whole = whole.reshape(parts, -1, 128)
            got = lax.all_to_all(whole, both, split_axis=0, concat_axis=0, tiled=True)
            got = jnp.sum(got, axis=0)
            small_grads[layer] = (got + plan.swap(got, "rep", 1)).reshape(-1)
        else:
            got = lax.psum_scatter(whole, both, scatter_dimension=0, tiled=False)
            small_grads[layer] = lax.psum(got, "rep")
    smalls = jnp.stack(small_grads)
    vec = smalls[:, :cut_one].reshape(LAYERS, VECTORS, small)
    qv = smalls[:, cut_one:cut_two].reshape(LAYERS, 2, small)
    fc1_b = smalls[:, cut_two:]
    if plan.fast:
        kinds = ("qkv", "sum", "fc1", "rows")
        shapes = (qkv_weight.shape, proj_weight.shape, fc1_weight.shape, fc2_weight.shape)
        qkv_g, proj_g, fc1_g, fc2_g = [
            finish(kinds[i], shapes[i], [weight_grads[layer][i] for layer in range(LAYERS)])
            for i in range(4)
        ]
    else:
        qkv_g, proj_g, fc1_g, fc2_g = [
            jnp.stack([weight_grads[layer][i] for layer in range(LAYERS)]) for i in range(4)
        ]
    return (
        output, grad[None], vec[:, 0], vec[:, 1], qkv_g, qv, proj_g, vec[:, 2], vec[:, 3],
        vec[:, 4], vec[:, 5], fc1_g, fc1_b, fc2_g, vec[:, 6], vec[:, 7],
    )


def solution(mesh):
    plan = Plan(mesh)
    tokens = P(("rep", "fsdp"), "seq", None)
    vector = P(None, ("fsdp", "seq"))
    matrix = P(None, ("fsdp", "seq"), None)
    pair = P(None, None, ("fsdp", "seq"))
    params = (
        vector, vector, matrix, pair, matrix, vector, vector,
        vector, vector, matrix, vector, matrix, vector, vector,
    )
    return jax.shard_map(
        partial(shards, plan),
        mesh=mesh,
        in_specs=(tokens, tokens) + params,
        out_specs=(tokens, tokens) + params,
        check_vma=False,
    )
```
